128 devices in a mesh: section: 4 (over x), dom: 32 (over z, y, core).
Axes of the slice: x: 4, y: 4, z: 4, core: 2. Of those that a mesh axis runs over, the one named last changes fastest.
Arguments:
- features: bfloat16 [2, 16384, 1024], P(None, 'dom'), may hold values from -6 to 6
- tiles: bfloat16 [2, 128, 12, 128, 128], P(None, 'dom'), may hold values from -0.15625 to 0.15625
- w_first: bfloat16 [4, 1024, 1024], P('section'), may hold values from -0.1875 to 0.1875
- w_second: bfloat16 [4, 1024, 1024], P('section'), may hold values from -0.1875 to 0.1875
- tile_block: int32 [2, 128, 12], replicated, may hold values from 0 to 255, as said below
Outputs:
- layer_outputs: bfloat16 [4, 2, 16384, 1024], P('section', None, 'dom')
The draws below stay inside these ranges and needn't reach their ends.
Inputs may be any that keep to these rules, and one draw needn't show every extreme that they name: `tile_block`: block row r belongs to partition r // 4 of a cycle of partitions. Entry [c, r, j] names a block of span c or an earlier span, owned by the partition of row r or by one of the two partitions beside it on the cycle. Among the 48 entries of one partition's block rows in one span, at most 6 name blocks of the partition one below and at most 6 name blocks of the partition one above, and one of these two counts is exactly 6 in every span and partition. Entries may repeat.
All inputs are finite; a program needn't handle non-finite values.
Results may differ from the reference program's by a relative error of at most 0.012.
Values may be sent and summed in bfloat16 or wider, within the bound.
No kernel may reach another device: no remote copies, remote signals or barrier semaphores. Data moves between devices by JAX's collectives and lax.ppermute only.
A program may use at most 128 MiB of HBM per device.

```python
import jax
import jax.numpy as jnp
from jax import lax

F = 1024
TILE = 128
NT = 12
SPANS = 2
BR = 4
LAYERS = 4
K = 6
NBC = 128
VERTS = 16384


def draw_group(key, span_id, target):
    part_count = NBC // BR
    tiles_row = BR * NT
    key_dir, key_rest, key_mix, key_span, key_row = jax.random.split(key, 5)
    full_dir = jax.random.randint(key_dir, (), 0, 2).astype(jnp.int32)
    rest_pool = jnp.where(jnp.arange(tiles_row) < K, 1 - full_dir, 2).astype(jnp.int32)
    rest_pool = jax.random.permutation(key_rest, rest_pool)[:tiles_row - K]
    directions = jnp.concatenate([jnp.full((K,), full_dir, jnp.int32), rest_pool])
    directions = jax.random.permutation(key_mix, directions)
    offset_val = jnp.where(directions == 0, -1, jnp.where(directions == 1, 1, 0))
    owner = (target + offset_val) % part_count
    source_span = jax.random.randint(key_span, (tiles_row,), 0, span_id + 1)
    row_pick = jax.random.randint(key_row, (tiles_row,), 0, BR)
    global_ids = source_span * NBC + owner * BR + row_pick
    return global_ids.astype(jnp.int32).reshape(BR, NT)


def draw_tile_block(key, part):
    part_count = NBC // BR
    keys = jax.random.split(jax.random.fold_in(key, 7), SPANS * part_count)
    span_ids = jnp.repeat(jnp.arange(SPANS), part_count).astype(jnp.int32)
    targets = jnp.tile(jnp.arange(part_count), SPANS).astype(jnp.int32)
    grouped = jax.vmap(draw_group)(keys, span_ids, targets)
    return grouped.reshape(SPANS, NBC, NT)


def levels(own_key, dims, shards, smallest, top_value):
    def one(dim, parts):
        steps = jax.random.uniform(jax.random.fold_in(jax.random.fold_in(own_key, 6), dim), (parts,), jnp.float32, smallest / len(shards), top_value / len(shards))
        return jnp.repeat(jnp.exp(steps), dims[dim] // parts).reshape((-1,) + (1,) * (len(dims) - dim - 1))

    factor_of = one(*shards[0])
    for cut in shards[1:]:
        factor_of = factor_of * one(*cut)
    return factor_of


def normal_values(own_key, extent, deviation, most, shards=(), kind=jnp.bfloat16):
    values = deviation * jax.random.normal(own_key, extent, jnp.float32)
    if shards:
        values = values * levels(own_key, extent, shards, -0.22, 0.18)
    return jnp.clip(values, -most, most).astype(kind)


def setup_inputs(seed: int = 0) -> dict:
    key_of = jax.random.split(jax.random.key(seed), 6)
    return {
        "features": normal_values(key_of[0], (SPANS, VERTS, F), 1.0, 6.0, ((1, 32),)),
        "tiles": normal_values(key_of[1], (SPANS, NBC, NT, TILE, TILE), (NT * TILE) ** -0.5, 0.15625, ((1, 32),)),
        "w_first": normal_values(key_of[2], (LAYERS, F, F), F ** -0.5, 0.1875, ((0, 4),)),
        "w_second": normal_values(key_of[3], (LAYERS, F, F), F ** -0.5, 0.1875, ((0, 4),)),
        "tile_block": draw_tile_block(jax.random.fold_in(key_of[5], 71), 0),
    }


def reference(features, tiles, w_first, w_second, tile_block):
    current = features
    flat_ids = tile_block.reshape(-1, NT)
    flat_tiles = tiles.reshape(-1, NT, TILE, TILE)
    results = []
    for layer_idx in range(LAYERS):
        blocks = current.reshape(-1, TILE, F)

        def one_row(packed):
            block_ids, row_tiles = packed
            gathered = jnp.take(blocks, block_ids, axis=0)
            summed = jnp.einsum("jab,jbf->af", row_tiles.astype(jnp.float32), gathered.astype(jnp.float32))
            return summed.astype(jnp.bfloat16)

        agg_rows = lax.map(one_row, (flat_ids, flat_tiles)).reshape(-1, F)
        hidden = jax.nn.relu(jnp.dot(agg_rows, w_first[layer_idx], preferred_element_type=jnp.float32)).astype(jnp.bfloat16)
        updated = current.reshape(-1, F).astype(jnp.float32) + jnp.dot(hidden, w_second[layer_idx], preferred_element_type=jnp.float32)
        current = updated.astype(jnp.bfloat16).reshape(current.shape)
        results.append(current)
    return jnp.stack(results)
```

```python
import functools

import jax
import jax.numpy as jnp
from jax import lax
from jax.experimental import pallas as pl
from jax.experimental.pallas import tpu as pltpu
from jax.sharding import PartitionSpec as P


ANY = pl.BlockSpec(memory_space=pl.ANY)
SMEM = pl.BlockSpec(memory_space=pltpu.SMEM)


def entry(ids_ref, me, parts, nbc, blk_rows, span, row, j):
    block = ids_ref[span, row, j]
    within = block % nbc
    rel = (within // blk_rows - me + parts) % parts
    local = block // nbc * blk_rows + within % blk_rows
    on_chip = jnp.where(me % 2 == 0, 1, parts - 1)
    kind = jnp.where(rel == 0, 0, jnp.where(rel == on_chip, 1, 2))
    return local, kind


def early_kernel(span, parts, nbc, n_src, meta_ref, ids_ref, tiles_ref, *refs):
    srcs = refs[:n_src]
    acc_ref, buf, tbuf, src_sem, tile_sem = refs[n_src:]
    me = meta_ref[0]
    blk_rows, n_tiles, tile_len, _ = tbuf.shape
    half = n_src // 2
    copies = [pltpu.make_async_copy(tiles_ref.at[span], tbuf, tile_sem)]
    for i, src in enumerate(srcs):
        copies.append(pltpu.make_async_copy(src, buf.at[pl.ds(i, 1)], src_sem.at[i]))
    for copy in copies:
        copy.start()
    for copy in copies:
        copy.wait()

    def one_row(row, carry):
        total = None
        for pair in range(n_tiles // 2):
            lhs, rhs = [], []
            for j in (2 * pair, 2 * pair + 1):
                local, kind = entry(ids_ref, me, parts, nbc, blk_rows, span, row, j)
                slot = jnp.where(kind == 2, 0, jnp.where(kind == 1, half + local, local))
                tile = tbuf[row, j]
                lhs.append(jnp.where(kind == 2, jnp.zeros_like(tile), tile))
                rhs.append(buf[slot])
            part = jnp.dot(
                jnp.concatenate(lhs, axis=1),
                jnp.concatenate(rhs, axis=0),
                preferred_element_type=jnp.float32,
            )
            total = part if total is None else total + part
        acc_ref[row] = total
        return carry

    lax.fori_loop(0, blk_rows, one_row, 0)


def late_kernel(span, parts, nbc, n_cross, n_rows, meta_ref, ids_ref, tiles_ref, acc_ref, *refs):
    crosses = refs[:n_cross]
    resid = refs[n_cross : n_cross + n_rows]
    wa_ref, wb_ref = refs[n_cross + n_rows : n_cross + n_rows + 2]
    outs = refs[n_cross + n_rows + 2 : n_cross + 2 * n_rows + 2]
    cbuf, tbuf, accbuf, rbuf, w1buf, w2buf, c_sem, r_sem, sem = refs[n_cross + 2 * n_rows + 2 :]
    me = meta_ref[0]
    flip = meta_ref[1]
    blk_rows, n_tiles, tile_len, _ = tbuf.shape
    first = [
        pltpu.make_async_copy(src, cbuf.at[pl.ds(i, 1)], c_sem.at[i]) for i, src in enumerate(crosses)
    ]
    first.append(pltpu.make_async_copy(tiles_ref.at[span], tbuf, sem.at[0]))
    first.append(pltpu.make_async_copy(acc_ref, accbuf, sem.at[1]))
    for copy in first:
        copy.start()

    @pl.when(flip == 0)
    def _():
        pltpu.make_async_copy(wa_ref, w1buf, sem.at[2]).start()
        pltpu.make_async_copy(wb_ref, w2buf, sem.at[3]).start()

    @pl.when(flip != 0)
    def _():
        pltpu.make_async_copy(wb_ref, w1buf, sem.at[2]).start()
        pltpu.make_async_copy(wa_ref, w2buf, sem.at[3]).start()

    second = [
        pltpu.make_async_copy(src, rbuf.at[pl.ds(i, 1)], r_sem.at[i]) for i, src in enumerate(resid)
    ]
    for copy in second:
        copy.start()
    for copy in first:
        copy.wait()

    def one_entry(e, carry):
        row = e // n_tiles
        j = e % n_tiles
        local, kind = entry(ids_ref, me, parts, nbc, blk_rows, span, row, j)

        @pl.when(kind == 2)
        def _():
            accbuf[row] += jnp.dot(tbuf[row, j], cbuf[local], preferred_element_type=jnp.float32)

        return carry

    lax.fori_loop(0, blk_rows * n_tiles, one_entry, 0)
    pltpu.make_async_copy(wa_ref, w1buf, sem.at[2]).wait()
    for copy in second:
        copy.wait()
    pltpu.make_async_copy(wb_ref, w2buf, sem.at[3]).wait()
    step = 2
    feat = accbuf.shape[2]
    for row in range(0, n_rows, step):
        agg = accbuf[row : row + step].reshape(step * tile_len, feat).astype(jnp.bfloat16)
        hidden = jnp.dot(agg, w1buf[...], preferred_element_type=jnp.float32)
        hidden = jnp.maximum(hidden, 0.0).astype(jnp.bfloat16)
        more = jnp.dot(hidden, w2buf[...], preferred_element_type=jnp.float32)
        more = more.reshape(step, tile_len, feat)
        for k in range(step):
            outs[row + k][0] = (rbuf[row + k].astype(jnp.float32) + more[k]).astype(jnp.bfloat16)


def early(span, parts, meta, ids, tiles, srcs):
    _, blk_rows, n_tiles, tile_len, _ = tiles.shape
    feat = srcs[0].shape[-1]
    nbc = parts * blk_rows
    n_src = len(srcs)
    return pl.pallas_call(
        functools.partial(early_kernel, span, parts, nbc, n_src),
        out_shape=jax.ShapeDtypeStruct((blk_rows, tile_len, feat), jnp.float32),
        in_specs=[SMEM, SMEM, ANY] + [ANY] * n_src,
        out_specs=pl.BlockSpec(memory_space=pltpu.VMEM),
        scratch_shapes=[
            pltpu.VMEM((n_src, tile_len, feat), jnp.bfloat16),
            pltpu.VMEM((blk_rows, n_tiles, tile_len, tile_len), jnp.bfloat16),
            pltpu.SemaphoreType.DMA((n_src,)),
            pltpu.SemaphoreType.DMA,
        ],
        compiler_params=pltpu.CompilerParams(vmem_limit_bytes=24 * 2**20),
        cost_estimate=pl.CostEstimate(
            flops=2 * blk_rows * n_tiles * tile_len * tile_len * feat,
            bytes_accessed=8 * 2**20,
            transcendentals=0,
        ),
        name=f"early{span}",
    )(meta, ids, tiles, *srcs)


def late(span, parts, meta, ids, tiles, acc, crosses, resid, wa, wb):
    _, blk_rows, n_tiles, tile_len, _ = tiles.shape
    feat = acc.shape[-1]
    nbc = parts * blk_rows
    n_cross = len(crosses)
    n_rows = len(resid)
    return pl.pallas_call(
        functools.partial(late_kernel, span, parts, nbc, n_cross, n_rows),
        out_shape=[jax.ShapeDtypeStruct((1, tile_len, feat), jnp.bfloat16)] * n_rows,
        in_specs=[SMEM, SMEM] + [ANY] * (2 + n_cross + n_rows + 2),
        out_specs=[pl.BlockSpec(memory_space=pltpu.VMEM)] * n_rows,
        scratch_shapes=[
            pltpu.VMEM((n_cross, tile_len, feat), jnp.bfloat16),
            pltpu.VMEM((blk_rows, n_tiles, tile_len, tile_len), jnp.bfloat16),
            pltpu.VMEM((blk_rows, tile_len, feat), jnp.float32),
            pltpu.VMEM((n_rows, tile_len, feat), jnp.bfloat16),
            pltpu.VMEM((feat, feat), jnp.bfloat16),
            pltpu.VMEM((feat, feat), jnp.bfloat16),
            pltpu.SemaphoreType.DMA((n_cross,)),
            pltpu.SemaphoreType.DMA((n_rows,)),
            pltpu.SemaphoreType.DMA((4,)),
        ],
        compiler_params=pltpu.CompilerParams(vmem_limit_bytes=28 * 2**20),
        cost_estimate=pl.CostEstimate(
            flops=4 * n_rows * tile_len * feat * feat,
            bytes_accessed=10 * 2**20,
            transcendentals=0,
        ),
        name=f"late{span}",
    )(meta, ids, tiles, acc, *crosses, *resid, wa, wb)


def on_device(features, tiles, w_first, w_second, tile_block):
    spans, row_count, feat = features.shape
    _, blk_rows, n_tiles, tile_len, _ = tiles.shape
    sections = lax.axis_size("section")
    parts = lax.axis_size("dom")
    section = lax.axis_index("section")
    me = lax.axis_index("dom")
    last = sections - 1
    swap = [(p, p ^ 1) for p in range(parts)]
    cross = [(p, (p + 1) % parts if p % 2 else (p - 1) % parts) for p in range(parts)]

    def move(blocks, axis, pairs):
        return [lax.ppermute(b, axis, pairs) for b in blocks]

    ids = lax.dynamic_slice_in_dim(tile_block, me * blk_rows, blk_rows, 1)
    meta_own = jnp.stack([me, jnp.zeros_like(me)]).astype(jnp.int32)
    meta_got = jnp.stack([me, me % 2]).astype(jnp.int32)
    w_first, w_second = w_first[0], w_second[0]

    piece = jnp.where(me % 2 == 0, w_first, w_second)
    got = lax.ppermute(piece, "section", [(1, 0), (last - 1, last)])
    other = lax.ppermute(got, "dom", swap)

    def unit(span, own, chip, over, wa, wb, meta):
        srcs = sum(own[: span + 1], []) + sum(chip[: span + 1], [])
        acc = early(span, parts, meta, ids, tiles, srcs)
        return list(late(span, parts, meta, ids, tiles, acc, sum(over[: span + 1], []), own[span], wa, wb))

    def layer(h, wa, wb, meta):
        chip = [move(b, "dom", swap) for b in h]
        over = [move(b, "dom", cross) for b in h]
        return [unit(s, h, chip, over, wa, wb, meta) for s in range(spans)]

    blocks = features.reshape(spans, blk_rows, 1, tile_len, feat)
    h0 = [[blocks[s, r] for r in range(blk_rows)] for s in range(spans)]
    h1 = layer(h0, w_first, w_second, meta_own)
    h2 = layer(h1, got, other, meta_got)
    hop = [move(b, "section", [(0, last)]) for b in h2]
    out2 = [move(b, "section", [(0, 1)]) for b in h2]
    h3 = layer(hop, got, other, meta_got)
    out3 = [move(b, "section", [(last, last - 1)]) for b in h3]
    h4 = layer(h3, w_first, w_second, meta_own)

    rows = []
    for s in range(spans):
        for r in range(blk_rows):
            mid = jnp.where(section == 1, out2[s][r], out3[s][r])
            mid = jnp.where(section == 0, h1[s][r], mid)
            rows.append(jnp.where(section == last, h4[s][r], mid))
    return jnp.concatenate(rows, axis=0).reshape(1, spans, row_count, feat)


def solution(mesh):
    placed = (
        P(None, "dom", None),
        P(None, "dom", None, None, None),
        P("section", None, None),
        P("section", None, None),
        P(),
    )
    return jax.shard_map(
        on_device,
        mesh=mesh,
        in_specs=placed,
        out_specs=P("section", None, "dom", None),
        check_vma=False,
    )
```

```python
import functools

import jax
import jax.numpy as jnp
from jax import lax
from jax.experimental import pallas as pl
from jax.experimental.pallas import tpu as pltpu
from jax.sharding import PartitionSpec as P


ANY = pl.BlockSpec(memory_space=pl.ANY)
SMEM = pl.BlockSpec(memory_space=pltpu.SMEM)
VMEM = pl.BlockSpec(memory_space=pltpu.VMEM)
HBM = pl.BlockSpec(memory_space=pltpu.HBM)
MIB = 2**20


def entry_tables(ids, me, parts, nbc):
    spans, blk_rows, n_tiles = ids.shape
    count = blk_rows * n_tiles
    ids = ids.reshape(spans, count)
    within = ids % nbc
    rel = (within // blk_rows - me + parts) % parts
    local = ids // nbc * blk_rows + within % blk_rows
    on_chip = jnp.where(me % 2 == 0, 1, parts - 1)
    across = (rel != 0) & (rel != on_chip)
    held = (1 + jnp.arange(spans, dtype=jnp.int32)[:, None]) * blk_rows
    slot = jnp.where(across, 0, jnp.where(rel == on_chip, held + local, local))
    near = jnp.stack([slot, jnp.where(across, 0, 1)], axis=1).astype(jnp.int32)
    order = jnp.arange(count, dtype=jnp.int32)
    before = (order[None, :] < order[:, None])[None]
    rank = jnp.sum(jnp.where(before & across[:, None, :], 1, 0), axis=2)
    chosen = across[:, None, :] & (rank[:, None, :] == order[None, :, None])
    place = jnp.sum(jnp.where(chosen, order[None, None, :], 0), axis=2)
    block = jnp.sum(jnp.where(chosen, local[:, None, :], 0), axis=2)
    total = jnp.sum(jnp.where(across, 1, 0), axis=1, keepdims=True) + jnp.zeros_like(place)
    far = jnp.stack([place, block, total], axis=1).astype(jnp.int32)
    return near, far


def early_kernel(span, n_src, near_ref, tiles_ref, *refs):
    srcs = refs[:n_src]
    acc_ref, buf, tbuf, src_sem, tile_sem = refs[n_src:]
    blk_rows, n_tiles, _, _ = tbuf.shape
    copies = [pltpu.make_async_copy(tiles_ref.at[span], tbuf, tile_sem)]
    for i, src in enumerate(srcs):
        size = buf.shape[0] // n_src
        rows = pl.ds(i * size, size)
        copies.append(pltpu.make_async_copy(src.at[pl.ds(0, size)], buf.at[rows], src_sem.at[i]))
    for copy in copies:
        copy.start()
    for copy in copies:
        copy.wait()

    def one_row(row, carry):
        total = None
        for pair in range(n_tiles // 2):
            lhs, rhs = [], []
            for j in (2 * pair, 2 * pair + 1):
                e = row * n_tiles + j
                tile = tbuf[row, j]
                lhs.append(jnp.where(near_ref[span, 1, e] == 0, jnp.zeros_like(tile), tile))
                rhs.append(buf[near_ref[span, 0, e]])
            part = jnp.dot(
                jnp.concatenate(lhs, axis=1),
                jnp.concatenate(rhs, axis=0),
                preferred_element_type=jnp.float32,
            )
            total = part if total is None else total + part
        acc_ref[row] = total
        return carry

    lax.fori_loop(0, blk_rows, one_row, 0)


def pick_kernel(n_got, meta_ref, *refs):
    got_refs = refs[:n_got]
    w1_ref, w2_ref, sem = refs[n_got:]
    feat = w1_ref.shape[0]
    mid = feat // 2
    mode = meta_ref[1]

    def fetch(one, two):
        for part, dst, k in ((one, w1_ref, 0), (two, w2_ref, 1)):
            for src, rows in part:
                pltpu.make_async_copy(src, dst.at[rows], sem.at[k]).start()

    def halves(a, b):
        return [(a, pl.ds(0, mid)), (b, pl.ds(mid, mid))]

    def shards(a, b):
        z = meta_ref[0]
        quarter = a.shape[0] // 4
        part = []
        for k, away in enumerate((0, 3, 1, 2)):
            start = pl.multiple_of((z + away) % 4 * quarter, quarter)
            part.append((a.at[pl.ds(k * quarter, quarter)], pl.ds(start, quarter)))
        return part + [(b, pl.ds(4 * quarter, feat - 4 * quarter))]

    choices = []
    for at in range(0, n_got, 4):
        form = halves if at < 8 else shards
        one, two = form(*got_refs[at : at + 2]), form(*got_refs[at + 2 : at + 4])
        choices += [(at // 2, one, two), (at // 2 + 1, two, one)]
    for value, one, two in choices:
        pl.when(mode == value)(functools.partial(fetch, one, two))
    pltpu.make_async_copy(w1_ref, w1_ref, sem.at[0]).wait()
    pltpu.make_async_copy(w2_ref, w2_ref, sem.at[1]).wait()


def pick(meta, got):
    feat = got[0].shape[-1]
    shape = jax.ShapeDtypeStruct((feat, feat), jnp.bfloat16)
    return list(
        pl.pallas_call(
            functools.partial(pick_kernel, len(got)),
            out_shape=[shape, shape],
            in_specs=[SMEM] + [ANY] * len(got),
            out_specs=[VMEM, VMEM],
            scratch_shapes=[pltpu.SemaphoreType.DMA((2,))],
            compiler_params=pltpu.CompilerParams(vmem_limit_bytes=6 * MIB),
            cost_estimate=pl.CostEstimate(flops=0, bytes_accessed=8 * MIB, transcendentals=0),
            name="pick",
        )(meta, *got)
    )


CUT = 384


def mine_kernel(meta_ref, first_ref, second_ref, quarter_ref, rest_ref, a_ref, b_ref, sem):
    size = quarter_ref.shape[0]
    mid = a_ref.shape[0]

    def fetch(src):
        start = pl.multiple_of(meta_ref[0] * size, size)
        pltpu.make_async_copy(src.at[pl.ds(start, size)], quarter_ref, sem.at[0]).start()
        pltpu.make_async_copy(src.at[pl.ds(4 * size, rest_ref.shape[0])], rest_ref, sem.at[1]).start()
        pltpu.make_async_copy(src.at[pl.ds(0, mid)], a_ref, sem.at[2]).start()
        pltpu.make_async_copy(src.at[pl.ds(mid, mid)], b_ref, sem.at[3]).start()

    pl.when(meta_ref[1] == 0)(functools.partial(fetch, first_ref))
    pl.when(meta_ref[1] != 0)(functools.partial(fetch, second_ref))
    for k, dst in enumerate((quarter_ref, rest_ref, a_ref, b_ref)):
        pltpu.make_async_copy(dst, dst, sem.at[k]).wait()


def mine(meta, w_first, w_second):
    feat = w_first.shape[0]
    rows = (CUT // 4, feat - CUT, feat // 2, feat // 2)
    return pl.pallas_call(
        mine_kernel,
        out_shape=[jax.ShapeDtypeStruct((size, feat), jnp.bfloat16) for size in rows],
        in_specs=[SMEM, HBM, HBM],
        out_specs=[VMEM] * 4,
        scratch_shapes=[pltpu.SemaphoreType.DMA((4,))],
        compiler_params=pltpu.CompilerParams(vmem_limit_bytes=56 * MIB),
        cost_estimate=pl.CostEstimate(flops=0, bytes_accessed=8 * MIB, transcendentals=0),
        name="mine",
    )(meta, w_first, w_second)


def join_kernel(*refs):
    *parts, out_ref, sem = refs
    size = parts[0].shape[0]
    for k, part in enumerate(parts):
        pltpu.make_async_copy(part, out_ref.at[pl.ds(k * size, size)], sem).start()
    pltpu.make_async_copy(out_ref, out_ref, sem).wait()


def join(*parts):
    size, feat = parts[0].shape
    return pl.pallas_call(
        join_kernel,
        out_shape=jax.ShapeDtypeStruct((len(parts) * size, feat), jnp.bfloat16),
        in_specs=[ANY] * len(parts),
        out_specs=VMEM,
        scratch_shapes=[pltpu.SemaphoreType.DMA],
        compiler_params=pltpu.CompilerParams(vmem_limit_bytes=4 * MIB),
        cost_estimate=pl.CostEstimate(flops=0, bytes_accessed=2 * MIB, transcendentals=0),
        name="join",
    )(*parts)


def place_kernel(sizes, meta_ref, *refs):
    count = sum(len(one) for one in sizes)
    others = refs[:count]
    out_ref, buf, sem = refs[count + 1 :]
    at = 0
    for k, one in enumerate(sizes):
        mine_refs = others[at : at + len(one)]
        at += len(one)

        @pl.when(meta_ref[2] == k)
        def _():
            start = 0
            for src, size in zip(mine_refs, one):
                pltpu.make_async_copy(src, buf.at[pl.ds(start, size)], sem).start()
                start += size
            pltpu.make_async_copy(buf, buf, sem).wait()
            copy = pltpu.make_async_copy(buf, out_ref, sem)
            copy.start()
            copy.wait()


def place(meta, others, out):
    flat = sum(others, [])
    sizes = [[part.shape[0] for part in one] for one in others]
    return pl.pallas_call(
        functools.partial(place_kernel, sizes),
        out_shape=jax.ShapeDtypeStruct(out.shape, out.dtype),
        in_specs=[SMEM] + [ANY] * len(flat) + [HBM],
        out_specs=HBM,
        scratch_shapes=[pltpu.VMEM(out.shape, out.dtype), pltpu.SemaphoreType.DMA],
        input_output_aliases={len(flat) + 1: 0},
        compiler_params=pltpu.CompilerParams(vmem_limit_bytes=6 * MIB),
        cost_estimate=pl.CostEstimate(flops=0, bytes_accessed=4 * MIB, transcendentals=0),
        name="place",
    )(meta, *flat, out)


def late_kernel(span, n_cross, final, far_ref, meta_ref, tiles_ref, acc_ref, resid_ref, w1_ref, w2_ref, *refs):
    crosses = refs[:n_cross]
    out_ref, cacc, tb, t_sem, *more_refs = refs[n_cross + (1 if final and span else 0) :]
    obuf = more_refs[0] if final else out_ref
    blk_rows, tile_len, feat = cacc.shape
    n_tiles = tiles_ref.shape[2]
    total = jnp.minimum(far_ref[span, 2, 0], tb.shape[0])

    def tile_copy(k):
        e = far_ref[span, 0, k]
        return pltpu.make_async_copy(tiles_ref.at[span, e // n_tiles, e % n_tiles], tb.at[k], t_sem.at[k])

    def start_tile(k, carry):
        tile_copy(k).start()
        return carry

    lax.fori_loop(0, total, start_tile, 0)
    cacc[...] = jnp.zeros_like(cacc)

    def one_entry(k, carry):
        row = far_ref[span, 0, k] // n_tiles
        block = far_ref[span, 1, k]
        tile_copy(k).wait()
        for c, src in enumerate(crosses):

            @pl.when((len(crosses) == 1) | (block // blk_rows == c))
            def _():
                cacc[row] += jnp.dot(tb[k], src[block - c * blk_rows], preferred_element_type=jnp.float32)

        return carry

    lax.fori_loop(0, total, one_entry, 0)
    step = 2

    def one_part(i, carry):
        rows = pl.ds(i * step, step)
        first = (resid_ref.shape[0] // blk_rows - 1) * span * blk_rows
        from_rows = pl.ds(first + i * step, step)
        agg = (acc_ref[rows] + cacc[rows]).reshape(step * tile_len, feat).astype(jnp.bfloat16)
        hidden = jnp.dot(agg, w1_ref[...], preferred_element_type=jnp.float32)
        hidden = jnp.maximum(hidden, 0.0).astype(jnp.bfloat16)
        more = jnp.dot(hidden, w2_ref[...], preferred_element_type=jnp.float32)
        more = more.reshape(step, tile_len, feat)
        obuf[rows] = (resid_ref[from_rows].astype(jnp.float32) + more).astype(jnp.bfloat16)
        if final:
            dst = out_ref.at[pl.ds(span * blk_rows + i * step, step)]
            pltpu.make_async_copy(obuf.at[rows], dst, more_refs[1]).start()
        return carry

    parts = jnp.where(meta_ref[3] != 0, blk_rows // step, 0)
    lax.fori_loop(0, parts, one_part, 0)
    if final:

        @pl.when(meta_ref[3] != 0)
        def _():
            pltpu.make_async_copy(obuf, out_ref.at[pl.ds(span * blk_rows, blk_rows)], more_refs[1]).wait()


def early(span, near, tiles, srcs):
    _, blk_rows, n_tiles, tile_len, _ = tiles.shape
    feat = srcs[0].shape[-1]
    n_src = len(srcs)
    return pl.pallas_call(
        functools.partial(early_kernel, span, n_src),
        out_shape=jax.ShapeDtypeStruct((blk_rows, tile_len, feat), jnp.float32),
        in_specs=[SMEM, ANY] + [ANY] * n_src,
        out_specs=VMEM,
        scratch_shapes=[
            pltpu.VMEM((2 * (span + 1) * blk_rows, tile_len, feat), jnp.bfloat16),
            pltpu.VMEM((blk_rows, n_tiles, tile_len, tile_len), jnp.bfloat16),
            pltpu.SemaphoreType.DMA((n_src,)),
            pltpu.SemaphoreType.DMA,
        ],
        compiler_params=pltpu.CompilerParams(vmem_limit_bytes=14 * MIB),
        cost_estimate=pl.CostEstimate(
            flops=2 * blk_rows * n_tiles * tile_len * tile_len * feat,
            bytes_accessed=8 * MIB,
            transcendentals=0,
        ),
    )(near, tiles, *srcs)


FAR = 8


def late(span, far, meta, tiles, acc, resid, crosses, weights, final=False, prior=None):
    spans, blk_rows, _, tile_len, _ = tiles.shape
    feat = acc.shape[-1]
    tail = [] if prior is None else [prior]
    args = [far, meta, tiles, acc, resid, *weights, *crosses, *tail]
    out_rows = spans * blk_rows if final else blk_rows
    return pl.pallas_call(
        functools.partial(late_kernel, span, len(crosses), final),
        out_shape=jax.ShapeDtypeStruct((out_rows, tile_len, feat), jnp.bfloat16),
        in_specs=[SMEM, SMEM, ANY] + [VMEM] * (4 + len(crosses)) + [HBM] * len(tail),
        out_specs=HBM if final else VMEM,
        scratch_shapes=[
            pltpu.VMEM((blk_rows, tile_len, feat), jnp.float32),
            pltpu.VMEM((FAR, tile_len, tile_len), jnp.bfloat16),
            pltpu.SemaphoreType.DMA((FAR,)),
        ]
        + ([pltpu.VMEM((blk_rows, tile_len, feat), jnp.bfloat16), pltpu.SemaphoreType.DMA] if final else []),
        compiler_params=pltpu.CompilerParams(vmem_limit_bytes=14 * MIB),
        input_output_aliases={len(args) - 1: 0} if tail else {},
        cost_estimate=pl.CostEstimate(
            flops=4 * blk_rows * tile_len * feat * feat,
            bytes_accessed=8 * MIB,
            transcendentals=0,
        ),
    )(*args)


def after(value, *deps):
    return lax.optimization_barrier((value, *deps))[0]


def on_device(features, tiles, w_first, w_second, tile_block):
    spans, row_count, feat = features.shape
    _, blk_rows, _, tile_len, _ = tiles.shape
    parts = lax.axis_size("dom")
    section = lax.axis_index("section")
    me = lax.axis_index("dom")
    hub = lax.axis_size("section") - 1
    row_parts = parts // 4
    z = me // row_parts
    swap_pairs = [(p, p ^ 1) for p in range(parts)]
    cross_pairs = [(p, (p + 1) % parts if p % 2 else (p - 1) % parts) for p in range(parts)]

    def swap(value):
        return lax.ppermute(value, "dom", swap_pairs)

    def cross(value):
        return lax.ppermute(value, "dom", cross_pairs)

    def hop(value, pairs):
        return lax.ppermute(value, "section", pairs)

    def along_z(value, by):
        return lax.ppermute(value, "dom", [(p, (p + by * row_parts) % parts) for p in range(parts)])

    def sums(span, h, chip):
        return early(span, near, tiles, h[: span + 1] + chip[: span + 1])

    w_first, w_second = w_first[0], w_second[0]

    def meta(mode, active):
        return jnp.stack([z, mode + me % 2, section, active.astype(jnp.int32)]).astype(jnp.int32)

    is_hub = section == hub
    metas = [
        meta(jnp.where(section == 0, 0, jnp.where(is_hub, 4, 2)), section != 2),
        meta(jnp.where(section == 1, 0, 2), (section == 1) | is_hub),
        meta(jnp.zeros_like(me), is_hub),
        meta(jnp.zeros_like(me), is_hub),
    ]

    def layer(num, acc, h, over, weights):
        out, chip_out, over_out = [], [], []
        for s in range(spans):
            out.append(late(s, far, metas[num], tiles, acc[s], h[s], over[: s + 1], weights))
            chip_out.append(swap(out[s]))
            over_out.append(cross(out[s]))
        return out, chip_out, over_out, [sums(s, out, chip_out) for s in range(spans)]

    shard, rest, mine_a, mine_b = mine(metas[3], w_first, w_second)
    shard = hop(shard, [(0, hub)])
    start = features.reshape(spans * blk_rows, tile_len, feat)
    chip0 = swap(start)
    over0 = cross(start)
    zero_b = hop(rest, [(0, hub)])
    next_a = hop(mine_a, [(0, 1), (1, 2), (2, hub)])
    zero_a = join(shard, along_z(shard, 1), along_z(shard, -1), along_z(shard, 2))
    next_b = hop(mine_b, [(0, 1)])
    ids = lax.dynamic_slice_in_dim(tile_block, me * blk_rows, blk_rows, 1)
    near, far = entry_tables(ids, me, parts, parts * blk_rows)
    near, far, *metas = lax.optimization_barrier((near, far, *metas))

    acc = [sums(s, [start], [chip0]) for s in range(spans)]
    one_a = hop(after(next_a, *acc), [(2, hub)])
    one_b = hop(after(mine_b, *acc), [(1, hub)])
    two_b = hop(after(mine_b, *acc), [(2, hub)])
    kept = [mine_a, mine_b, swap(mine_a), swap(mine_b)]
    swap_next = [swap(after(next_a, *acc)), swap(after(next_b, *acc))]
    swap_zero = [swap(zero_a), swap(after(zero_b, *acc))]
    got = [*kept, next_a, next_b, *swap_next, zero_a, zero_b, *swap_zero]
    h1, _, over1, acc = layer(0, acc, [start] * spans, [over0], pick(metas[0], got))
    one_a, one_b = after(one_a, *acc), after(one_b, *acc)
    got = [*kept, one_a, one_b, swap(one_a), swap(one_b)]
    weights = pick(metas[1], got)

    h2, _, over2, acc = layer(1, acc, h1, over1, weights)
    two_b = after(two_b, *acc)
    got = [next_a, two_b, swap_next[0], swap(two_b)]
    weights = pick(metas[2], got)

    h3, _, over3, acc = layer(2, acc, h2, over2, weights)
    half = blk_rows // 2
    away = hop(h3[0][half:], [(hub, 0)])
    away = hop(away, [(0, 1)])
    away = hop(away, [(1, 2)])
    back = [hop(h3[0][:half], [(hub, 2)]), away, hop(h3[1], [(hub, 2)])]

    out = None
    for s in range(spans):
        out = late(s, far, metas[3], tiles, acc[s], h3[s], over3[: s + 1], [w_first, w_second], True, out)
    out = place(metas[3], [h1, h2, back], out)
    return out.reshape(1, spans, row_count, feat)


def solution(mesh):
    placed = (
        P(None, "dom", None),
        P(None, "dom", None, None, None),
        P("section", None, None),
        P("section", None, None),
        P(),
    )
    return jax.shard_map(
        on_device,
        mesh=mesh,
        in_specs=placed,
        out_specs=P("section", None, "dom", None),
        check_vma=False,
    )
```

```python
import functools

import jax
import jax.numpy as jnp
from jax import lax
from jax.experimental import pallas as pl
from jax.experimental.pallas import tpu as pltpu
from jax.sharding import PartitionSpec as P


ANY = pl.BlockSpec(memory_space=pl.ANY)
SMEM = pl.BlockSpec(memory_space=pltpu.SMEM)
VMEM = pl.BlockSpec(memory_space=pltpu.VMEM)
HBM = pl.BlockSpec(memory_space=pltpu.HBM)
MIB = 2**20


def entry_tables(ids, me, parts, nbc):
    spans, blk_rows, n_tiles = ids.shape
    count = blk_rows * n_tiles
    ids = ids.reshape(spans, count)
    within = ids % nbc
    rel = (within // blk_rows - me + parts) % parts
    local = ids // nbc * blk_rows + within % blk_rows
    on_chip = jnp.where(me % 2 == 0, 1, parts - 1)
    across = (rel != 0) & (rel != on_chip)
    held = (1 + jnp.arange(spans, dtype=jnp.int32)[:, None]) * blk_rows
    slot = jnp.where(across, 0, jnp.where(rel == on_chip, held + local, local))
    near = jnp.stack([slot, jnp.where(across, 0, 1)], axis=1).astype(jnp.int32)
    order = jnp.arange(count, dtype=jnp.int32)
    before = (order[None, :] < order[:, None])[None]
    rank = jnp.sum(jnp.where(before & across[:, None, :], 1, 0), axis=2)
    chosen = across[:, None, :] & (rank[:, None, :] == order[None, :, None])
    place = jnp.sum(jnp.where(chosen, order[None, None, :], 0), axis=2)
    block = jnp.sum(jnp.where(chosen, local[:, None, :], 0), axis=2)
    total = jnp.sum(jnp.where(across, 1, 0), axis=1, keepdims=True) + jnp.zeros_like(place)
    far = jnp.stack([place, block, total], axis=1).astype(jnp.int32)
    return near, far


def early_kernel(span, n_src, near_ref, tiles_ref, *refs):
    srcs = refs[:n_src]
    acc_ref, buf, tbuf, src_sem, tile_sem = refs[n_src:]
    blk_rows, n_tiles, _, _ = tbuf.shape
    copies = [pltpu.make_async_copy(tiles_ref.at[span], tbuf, tile_sem)]
    for i, src in enumerate(srcs):
        size = buf.shape[0] // n_src
        rows = pl.ds(i * size, size)
        copies.append(pltpu.make_async_copy(src.at[pl.ds(0, size)], buf.at[rows], src_sem.at[i]))
    for copy in copies:
        copy.start()
    for copy in copies:
        copy.wait()

    def one_row(row, carry):
        total = None
        for pair in range(n_tiles // 2):
            lhs, rhs = [], []
            for j in (2 * pair, 2 * pair + 1):
                e = row * n_tiles + j
                tile = tbuf[row, j]
                lhs.append(jnp.where(near_ref[span, 1, e] == 0, jnp.zeros_like(tile), tile))
                rhs.append(buf[near_ref[span, 0, e]])
            part = jnp.dot(
                jnp.concatenate(lhs, axis=1),
                jnp.concatenate(rhs, axis=0),
                preferred_element_type=jnp.float32,
            )
            total = part if total is None else total + part
        acc_ref[row] = total
        return carry

    lax.fori_loop(0, blk_rows, one_row, 0)


def pick_kernel(n_got, meta_ref, *refs):
    got_refs = refs[:n_got]
    w1_ref, w2_ref, sem = refs[n_got:]
    feat = w1_ref.shape[0]
    mid = feat // 2
    mode = meta_ref[1]

    def fetch(one, two):
        for part, dst, k in ((one, w1_ref, 0), (two, w2_ref, 1)):
            for src, rows in part:
                pltpu.make_async_copy(src, dst.at[rows], sem.at[k]).start()

    def halves(a, b):
        return [(a, pl.ds(0, mid)), (b, pl.ds(mid, mid))]

    def shards(a, b):
        z = meta_ref[0]
        quarter = a.shape[0] // 4
        part = []
        for k, away in enumerate((0, 3, 1, 2)):
            start = pl.multiple_of((z + away) % 4 * quarter, quarter)
            part.append((a.at[pl.ds(k * quarter, quarter)], pl.ds(start, quarter)))
        return part + [(b, pl.ds(4 * quarter, feat - 4 * quarter))]

    choices = []
    for at in range(0, n_got, 4):
        form = halves if at < 8 else shards
        one, two = form(*got_refs[at : at + 2]), form(*got_refs[at + 2 : at + 4])
        choices += [(at // 2, one, two), (at // 2 + 1, two, one)]
    for value, one, two in choices:
        pl.when(mode == value)(functools.partial(fetch, one, two))
    pltpu.make_async_copy(w1_ref, w1_ref, sem.at[0]).wait()
    pltpu.make_async_copy(w2_ref, w2_ref, sem.at[1]).wait()


def pick(meta, got):
    feat = got[0].shape[-1]
    shape = jax.ShapeDtypeStruct((feat, feat), jnp.bfloat16)
    return list(
        pl.pallas_call(
            functools.partial(pick_kernel, len(got)),
            out_shape=[shape, shape],
            in_specs=[SMEM] + [ANY] * len(got),
            out_specs=[VMEM, VMEM],
            scratch_shapes=[pltpu.SemaphoreType.DMA((2,))],
            compiler_params=pltpu.CompilerParams(vmem_limit_bytes=6 * MIB),
            cost_estimate=pl.CostEstimate(flops=0, bytes_accessed=8 * MIB, transcendentals=0),
            name="pick",
        )(meta, *got)
    )


CUT = 384


def mine_kernel(pieces, meta_ref, first_ref, second_ref, *refs):
    *outs, sem = refs

    def fetch(src):
        for k, ((start, per_z), dst) in enumerate(zip(pieces, outs)):
            size = dst.shape[0]
            rows = pl.ds(pl.multiple_of(meta_ref[0] * size, size) if per_z else start, size)
            pltpu.make_async_copy(src.at[rows], dst, sem.at[k]).start()

    pl.when(meta_ref[1] == 0)(functools.partial(fetch, first_ref))
    pl.when(meta_ref[1] != 0)(functools.partial(fetch, second_ref))
    for k, dst in enumerate(outs):
        pltpu.make_async_copy(dst, dst, sem.at[k]).wait()


def mine(meta, w_first, w_second, pieces):
    feat = w_first.shape[0]
    fixed = tuple((start or 0, start is None) for start, _ in pieces)
    return pl.pallas_call(
        functools.partial(mine_kernel, fixed),
        out_shape=[jax.ShapeDtypeStruct((size, feat), jnp.bfloat16) for _, size in pieces],
        in_specs=[SMEM, HBM, HBM],
        out_specs=[VMEM] * len(pieces),
        scratch_shapes=[pltpu.SemaphoreType.DMA((len(pieces),))],
        compiler_params=pltpu.CompilerParams(vmem_limit_bytes=52 * MIB),
        cost_estimate=pl.CostEstimate(flops=0, bytes_accessed=4 * MIB, transcendentals=0),
        name="mine",
    )(meta, w_first, w_second)


def join_kernel(*refs):
    *parts, out_ref, sem = refs
    size = parts[0].shape[0]
    for k, part in enumerate(parts):
        pltpu.make_async_copy(part, out_ref.at[pl.ds(k * size, size)], sem).start()
    pltpu.make_async_copy(out_ref, out_ref, sem).wait()


def join(*parts):
    size, feat = parts[0].shape
    return pl.pallas_call(
        join_kernel,
        out_shape=jax.ShapeDtypeStruct((len(parts) * size, feat), jnp.bfloat16),
        in_specs=[ANY] * len(parts),
        out_specs=VMEM,
        scratch_shapes=[pltpu.SemaphoreType.DMA],
        compiler_params=pltpu.CompilerParams(vmem_limit_bytes=4 * MIB),
        cost_estimate=pl.CostEstimate(flops=0, bytes_accessed=2 * MIB, transcendentals=0),
        name="join",
    )(*parts)


def place_kernel(sizes, meta_ref, *refs):
    count = sum(len(one) for one in sizes)
    others = refs[:count]
    out_ref, buf, sem = refs[count + 1 :]
    at = 0
    for k, one in enumerate(sizes):
        mine_refs = others[at : at + len(one)]
        at += len(one)

        @pl.when(meta_ref[2] == k)
        def _():
            start = 0
            for src, size in zip(mine_refs, one):
                pltpu.make_async_copy(src, buf.at[pl.ds(start, size)], sem).start()
                start += size
            pltpu.make_async_copy(buf, buf, sem).wait()
            copy = pltpu.make_async_copy(buf, out_ref, sem)
            copy.start()
            copy.wait()


def place(meta, others, out):
    flat = sum(others, [])
    sizes = [[part.shape[0] for part in one] for one in others]
    return pl.pallas_call(
        functools.partial(place_kernel, sizes),
        out_shape=jax.ShapeDtypeStruct(out.shape, out.dtype),
        in_specs=[SMEM] + [ANY] * len(flat) + [HBM],
        out_specs=HBM,
        scratch_shapes=[pltpu.VMEM(out.shape, out.dtype), pltpu.SemaphoreType.DMA],
        input_output_aliases={len(flat) + 1: 0},
        compiler_params=pltpu.CompilerParams(vmem_limit_bytes=6 * MIB),
        cost_estimate=pl.CostEstimate(flops=0, bytes_accessed=4 * MIB, transcendentals=0),
        name="place",
    )(meta, *flat, out)


def late_kernel(span, n_cross, final, far_ref, meta_ref, tiles_ref, acc_ref, resid_ref, w1_ref, w2_ref, *refs):
    crosses = refs[:n_cross]
    out_ref, cacc, tb, t_sem, *more_refs = refs[n_cross + (1 if final and span else 0) :]
    obuf = more_refs[0] if final else out_ref
    blk_rows, tile_len, feat = cacc.shape
    n_tiles = tiles_ref.shape[2]
    total = jnp.minimum(far_ref[span, 2, 0], tb.shape[0])

    def tile_copy(k):
        e = far_ref[span, 0, k]
        return pltpu.make_async_copy(tiles_ref.at[span, e // n_tiles, e % n_tiles], tb.at[k], t_sem.at[k])

    def start_tile(k, carry):
        tile_copy(k).start()
        return carry

    lax.fori_loop(0, total, start_tile, 0)
    cacc[...] = jnp.zeros_like(cacc)

    def one_entry(k, carry):
        row = far_ref[span, 0, k] // n_tiles
        block = far_ref[span, 1, k]
        tile_copy(k).wait()
        for c, src in enumerate(crosses):

            @pl.when((len(crosses) == 1) | (block // blk_rows == c))
            def _():
                cacc[row] += jnp.dot(tb[k], src[block - c * blk_rows], preferred_element_type=jnp.float32)

        return carry

    lax.fori_loop(0, total, one_entry, 0)
    step = 2

    def one_part(i, carry):
        rows = pl.ds(i * step, step)
        first = (resid_ref.shape[0] // blk_rows - 1) * span * blk_rows
        from_rows = pl.ds(first + i * step, step)
        agg = (acc_ref[rows] + cacc[rows]).reshape(step * tile_len, feat).astype(jnp.bfloat16)
        hidden = jnp.dot(agg, w1_ref[...], preferred_element_type=jnp.float32)
        hidden = jnp.maximum(hidden, 0.0).astype(jnp.bfloat16)
        more = jnp.dot(hidden, w2_ref[...], preferred_element_type=jnp.float32)
        more = more.reshape(step, tile_len, feat)
        obuf[rows] = (resid_ref[from_rows].astype(jnp.float32) + more).astype(jnp.bfloat16)
        if final:
            dst = out_ref.at[pl.ds(span * blk_rows + i * step, step)]
            pltpu.make_async_copy(obuf.at[rows], dst, more_refs[1]).start()
        return carry

    parts = jnp.where(meta_ref[3] != 0, blk_rows // step, 0)
    lax.fori_loop(0, parts, one_part, 0)
    if final:

        @pl.when(meta_ref[3] != 0)
        def _():
            pltpu.make_async_copy(obuf, out_ref.at[pl.ds(span * blk_rows, blk_rows)], more_refs[1]).wait()


def early(span, near, tiles, srcs):
    _, blk_rows, n_tiles, tile_len, _ = tiles.shape
    feat = srcs[0].shape[-1]
    n_src = len(srcs)
    return pl.pallas_call(
        functools.partial(early_kernel, span, n_src),
        out_shape=jax.ShapeDtypeStruct((blk_rows, tile_len, feat), jnp.float32),
        in_specs=[SMEM, ANY] + [ANY] * n_src,
        out_specs=VMEM,
        scratch_shapes=[
            pltpu.VMEM((2 * (span + 1) * blk_rows, tile_len, feat), jnp.bfloat16),
            pltpu.VMEM((blk_rows, n_tiles, tile_len, tile_len), jnp.bfloat16),
            pltpu.SemaphoreType.DMA((n_src,)),
            pltpu.SemaphoreType.DMA,
        ],
        compiler_params=pltpu.CompilerParams(vmem_limit_bytes=14 * MIB),
        cost_estimate=pl.CostEstimate(
            flops=2 * blk_rows * n_tiles * tile_len * tile_len * feat,
            bytes_accessed=8 * MIB,
            transcendentals=0,
        ),
    )(near, tiles, *srcs)


FAR = 8


def late(span, far, meta, tiles, acc, resid, crosses, weights, final=False, prior=None):
    spans, blk_rows, _, tile_len, _ = tiles.shape
    feat = acc.shape[-1]
    tail = [] if prior is None else [prior]
    args = [far, meta, tiles, acc, resid, *weights, *crosses, *tail]
    out_rows = spans * blk_rows if final else blk_rows
    return pl.pallas_call(
        functools.partial(late_kernel, span, len(crosses), final),
        out_shape=jax.ShapeDtypeStruct((out_rows, tile_len, feat), jnp.bfloat16),
        in_specs=[SMEM, SMEM, ANY] + [VMEM] * (4 + len(crosses)) + [HBM] * len(tail),
        out_specs=HBM if final else VMEM,
        scratch_shapes=[
            pltpu.VMEM((blk_rows, tile_len, feat), jnp.float32),
            pltpu.VMEM((FAR, tile_len, tile_len), jnp.bfloat16),
            pltpu.SemaphoreType.DMA((FAR,)),
        ]
        + ([pltpu.VMEM((blk_rows, tile_len, feat), jnp.bfloat16), pltpu.SemaphoreType.DMA] if final else []),
        compiler_params=pltpu.CompilerParams(vmem_limit_bytes=14 * MIB),
        input_output_aliases={len(args) - 1: 0} if tail else {},
        cost_estimate=pl.CostEstimate(
            flops=4 * blk_rows * tile_len * feat * feat,
            bytes_accessed=8 * MIB,
            transcendentals=0,
        ),
    )(*args)


def after(value, *deps):
    return lax.optimization_barrier((value, *deps))[0]


def on_device(features, tiles, w_first, w_second, tile_block):
    spans, row_count, feat = features.shape
    _, blk_rows, _, tile_len, _ = tiles.shape
    parts = lax.axis_size("dom")
    section = lax.axis_index("section")
    me = lax.axis_index("dom")
    hub = lax.axis_size("section") - 1
    row_parts = parts // 4
    z = me // row_parts
    swap_pairs = [(p, p ^ 1) for p in range(parts)]
    cross_pairs = [(p, (p + 1) % parts if p % 2 else (p - 1) % parts) for p in range(parts)]

    def swap(value):
        return lax.ppermute(value, "dom", swap_pairs)

    def cross(value):
        return lax.ppermute(value, "dom", cross_pairs)

    def hop(value, pairs):
        return lax.ppermute(value, "section", pairs)

    def along_z(value, by):
        return lax.ppermute(value, "dom", [(p, (p + by * row_parts) % parts) for p in range(parts)])

    def sums(span, h, chip):
        return early(span, near, tiles, h[: span + 1] + chip[: span + 1])

    w_first, w_second = w_first[0], w_second[0]

    def meta(mode, active):
        return jnp.stack([z, mode + me % 2, section, active.astype(jnp.int32)]).astype(jnp.int32)

    is_hub = section == hub
    metas = [
        meta(jnp.where(section == 0, 0, jnp.where(is_hub, 4, 2)), section != 2),
        meta(jnp.where(section == 1, 0, 2), (section == 1) | is_hub),
        meta(jnp.zeros_like(me), is_hub),
        meta(jnp.zeros_like(me), is_hub),
    ]

    def layer(num, acc, h, over, weights):
        out, chip_out, over_out = [], [], []
        for s in range(spans):
            out.append(late(s, far, metas[num], tiles, acc[s], h[s], over[: s + 1], weights))
            chip_out.append(swap(out[s]))
            over_out.append(cross(out[s]))
        return out, chip_out, over_out, [sums(s, out, chip_out) for s in range(spans)]

    shard, rest = mine(metas[3], w_first, w_second, [(None, CUT // 4), (CUT, feat - CUT)])
    shard = hop(shard, [(0, hub)])
    zero_b = hop(rest, [(0, hub)])
    mine_a, mine_b = mine(metas[3], w_first, w_second, [(0, feat // 2), (feat // 2, feat // 2)])
    start = features.reshape(spans * blk_rows, tile_len, feat)
    chip0 = swap(start)
    over0 = [cross(start[s * blk_rows : (s + 1) * blk_rows]) for s in range(spans)]
    next_a = hop(mine_a, [(0, 1), (1, 2), (2, hub)])
    zero_a = join(shard, along_z(shard, 1), along_z(shard, -1), along_z(shard, 2))
    next_b = hop(mine_b, [(0, 1)])
    ids = lax.dynamic_slice_in_dim(tile_block, me * blk_rows, blk_rows, 1)
    near, far = entry_tables(ids, me, parts, parts * blk_rows)
    near, far, *metas = lax.optimization_barrier((near, far, *metas))

    acc = [sums(s, [start], [chip0]) for s in range(spans)]
    one_a = hop(after(next_a, *acc), [(2, hub)])
    one_b = hop(after(mine_b, *acc), [(1, hub)])
    two_b = hop(after(mine_b, *acc), [(2, hub)])
    kept = [mine_a, mine_b, swap(mine_a), swap(mine_b)]
    swap_next = [swap(next_a), swap(next_b)]
    swap_zero = [swap(zero_a), swap(zero_b)]
    got = [*kept, next_a, next_b, *swap_next, zero_a, zero_b, *swap_zero]
    h1, _, over1, acc = layer(0, acc, [start] * spans, over0, pick(metas[0], got))
    one_a, one_b = after(one_a, h1[1]), after(one_b, h1[1])
    got = [*kept, one_a, one_b, swap(one_a), swap(one_b)]
    weights = pick(metas[1], got)

    h2, _, over2, acc = layer(1, acc, h1, over1, weights)
    two_b = after(two_b, h2[1])
    got = [next_a, two_b, swap_next[0], swap(two_b)]
    weights = pick(metas[2], got)

    h3, _, over3, acc = layer(2, acc, h2, over2, weights)
    back = [hop(h3[s], [(hub, 2)]) for s in range(spans)]

    out = None
    for s in range(spans):
        out = late(s, far, metas[3], tiles, acc[s], h3[s], over3[: s + 1], [w_first, w_second], True, out)
    out = place(metas[3], [h1, h2, back], out)
    return out.reshape(1, spans, row_count, feat)


def solution(mesh):
    placed = (
        P(None, "dom", None),
        P(None, "dom", None, None, None),
        P("section", None, None),
        P("section", None, None),
        P(),
    )
    return jax.shard_map(
        on_device,
        mesh=mesh,
        in_specs=placed,
        out_specs=P("section", None, "dom", None),
        check_vma=False,
    )
```

```python
import functools

import jax
import jax.numpy as jnp
from jax import lax
from jax.experimental import pallas as pl
from jax.experimental.pallas import tpu as pltpu
from jax.sharding import PartitionSpec as P


ANY = pl.BlockSpec(memory_space=pl.ANY)
SMEM = pl.BlockSpec(memory_space=pltpu.SMEM)
VMEM = pl.BlockSpec(memory_space=pltpu.VMEM)
HBM = pl.BlockSpec(memory_space=pltpu.HBM)
MIB = 2**20


def entry_tables(ids, me, parts, nbc):
    spans, blk_rows, n_tiles = ids.shape
    count = blk_rows * n_tiles
    ids = ids.reshape(spans, count)
    within = ids % nbc
    rel = (within // blk_rows - me + parts) % parts
    local = ids // nbc * blk_rows + within % blk_rows
    on_chip = jnp.where(me % 2 == 0, 1, parts - 1)
    across = (rel != 0) & (rel != on_chip)
    held = (1 + jnp.arange(spans, dtype=jnp.int32)[:, None]) * blk_rows
    slot = jnp.where(across, 0, jnp.where(rel == on_chip, held + local, local))
    near = jnp.stack([slot, jnp.where(across, 0, 1)], axis=1).astype(jnp.int32)
    order = jnp.arange(count, dtype=jnp.int32)
    before = (order[None, :] < order[:, None])[None]
    rank = jnp.sum(jnp.where(before & across[:, None, :], 1, 0), axis=2)
    chosen = across[:, None, :] & (rank[:, None, :] == order[None, :, None])
    place = jnp.sum(jnp.where(chosen, order[None, None, :], 0), axis=2)
    block = jnp.sum(jnp.where(chosen, local[:, None, :], 0), axis=2)
    total = jnp.sum(jnp.where(across, 1, 0), axis=1, keepdims=True) + jnp.zeros_like(place)
    far = jnp.stack([place, block, total], axis=1).astype(jnp.int32)
    return near, far


def early_kernel(span, n_src, near_ref, tiles_ref, *refs):
    srcs = refs[:n_src]
    acc_ref, buf, tbuf, src_sem, tile_sem = refs[n_src:]
    blk_rows, n_tiles, _, _ = tbuf.shape
    copies = [pltpu.make_async_copy(tiles_ref.at[span], tbuf, tile_sem)]
    for i, src in enumerate(srcs):
        size = buf.shape[0] // n_src
        rows = pl.ds(i * size, size)
        copies.append(pltpu.make_async_copy(src.at[pl.ds(0, size)], buf.at[rows], src_sem.at[i]))
    for copy in copies:
        copy.start()
    for copy in copies:
        copy.wait()

    def one_row(row, carry):
        total = None
        for pair in range(n_tiles // 2):
            lhs, rhs = [], []
            for j in (2 * pair, 2 * pair + 1):
                e = row * n_tiles + j
                tile = tbuf[row, j]
                lhs.append(jnp.where(near_ref[span, 1, e] == 0, jnp.zeros_like(tile), tile))
                rhs.append(buf[near_ref[span, 0, e]])
            part = jnp.dot(
                jnp.concatenate(lhs, axis=1),
                jnp.concatenate(rhs, axis=0),
                preferred_element_type=jnp.float32,
            )
            total = part if total is None else total + part
        acc_ref[row] = total
        return carry

    lax.fori_loop(0, blk_rows, one_row, 0)


def pick_kernel(n_got, meta_ref, *refs):
    got_refs = refs[:n_got]
    w1_ref, w2_ref, sem = refs[n_got:]
    feat = w1_ref.shape[0]
    mid = feat // 2
    mode = meta_ref[1]

    def fetch(one, two):
        for part, dst, k in ((one, w1_ref, 0), (two, w2_ref, 1)):
            for src, rows in part:
                pltpu.make_async_copy(src, dst.at[rows], sem.at[k]).start()

    def halves(a, b):
        return [(a, pl.ds(0, mid)), (b, pl.ds(mid, mid))]

    def shards(a, b):
        z = meta_ref[0]
        quarter = a.shape[0] // 3
        part = []
        for src, k, away in ((a, 0, 0), (a, 1, 3), (a, 2, 1), (b, 0, 2)):
            start = pl.multiple_of((z + away) % 4 * quarter, quarter)
            part.append((src.at[pl.ds(k * quarter, quarter)], pl.ds(start, quarter)))
        size = feat - 4 * quarter
        return part + [(b.at[pl.ds(quarter, size)], pl.ds(4 * quarter, size))]

    choices = []
    for at in range(0, n_got, 4):
        form = halves if at < 8 else shards
        one, two = form(*got_refs[at : at + 2]), form(*got_refs[at + 2 : at + 4])
        choices += [(at // 2, one, two), (at // 2 + 1, two, one)]
    for value, one, two in choices:
        pl.when(mode == value)(functools.partial(fetch, one, two))
    pltpu.make_async_copy(w1_ref, w1_ref, sem.at[0]).wait()
    pltpu.make_async_copy(w2_ref, w2_ref, sem.at[1]).wait()


def pick(meta, got):
    feat = got[0].shape[-1]
    shape = jax.ShapeDtypeStruct((feat, feat), jnp.bfloat16)
    return list(
        pl.pallas_call(
            functools.partial(pick_kernel, len(got)),
            out_shape=[shape, shape],
            in_specs=[SMEM] + [ANY] * len(got),
            out_specs=[VMEM, VMEM],
            scratch_shapes=[pltpu.SemaphoreType.DMA((2,))],
            compiler_params=pltpu.CompilerParams(vmem_limit_bytes=6 * MIB),
            cost_estimate=pl.CostEstimate(flops=0, bytes_accessed=8 * MIB, transcendentals=0),
            name="pick",
        )(meta, *got)
    )


CUT = 768


def mine_kernel(pieces, meta_ref, first_ref, second_ref, *refs):
    *outs, sem = refs

    def fetch(src):
        for k, (ranges, dst) in enumerate(zip(pieces, outs)):
            at = 0
            for start, away, size in ranges:
                if away is not None:
                    start = pl.multiple_of((meta_ref[0] + away) % 4 * size, size)
                pltpu.make_async_copy(src.at[pl.ds(start, size)], dst.at[pl.ds(at, size)], sem.at[k]).start()
                at += size

    pl.when(meta_ref[1] == 0)(functools.partial(fetch, first_ref))
    pl.when(meta_ref[1] != 0)(functools.partial(fetch, second_ref))
    for k, dst in enumerate(outs):
        pltpu.make_async_copy(dst, dst, sem.at[k]).wait()


def mine(meta, w_first, w_second, pieces):
    feat = w_first.shape[0]
    shapes = [jax.ShapeDtypeStruct((sum(r[2] for r in one), feat), jnp.bfloat16) for one in pieces]
    return pl.pallas_call(
        functools.partial(mine_kernel, pieces),
        out_shape=shapes,
        in_specs=[SMEM, HBM, HBM],
        out_specs=[VMEM] * len(pieces),
        scratch_shapes=[pltpu.SemaphoreType.DMA((len(pieces),))],
        compiler_params=pltpu.CompilerParams(vmem_limit_bytes=52 * MIB),
        cost_estimate=pl.CostEstimate(flops=0, bytes_accessed=4 * MIB, transcendentals=0),
        name="mine",
    )(meta, w_first, w_second)


def join_kernel(*refs):
    *parts, out_ref, sem = refs
    size = parts[0].shape[0]
    for k, part in enumerate(parts):
        pltpu.make_async_copy(part, out_ref.at[pl.ds(k * size, size)], sem).start()
    pltpu.make_async_copy(out_ref, out_ref, sem).wait()


def join(*parts):
    size, feat = parts[0].shape
    return pl.pallas_call(
        join_kernel,
        out_shape=jax.ShapeDtypeStruct((len(parts) * size, feat), jnp.bfloat16),
        in_specs=[ANY] * len(parts),
        out_specs=VMEM,
        scratch_shapes=[pltpu.SemaphoreType.DMA],
        compiler_params=pltpu.CompilerParams(vmem_limit_bytes=4 * MIB),
        cost_estimate=pl.CostEstimate(flops=0, bytes_accessed=2 * MIB, transcendentals=0),
        name="join",
    )(*parts)


def place_kernel(sizes, meta_ref, *refs):
    count = sum(len(one) for one in sizes)
    others = refs[:count]
    out_ref, buf, sem = refs[count + 1 :]
    at = 0
    for k, one in enumerate(sizes):
        mine_refs = others[at : at + len(one)]
        at += len(one)

        @pl.when(meta_ref[2] == k)
        def _():
            start = 0
            for src, size in zip(mine_refs, one):
                pltpu.make_async_copy(src, buf.at[pl.ds(start, size)], sem).start()
                start += size
            pltpu.make_async_copy(buf, buf, sem).wait()
            copy = pltpu.make_async_copy(buf, out_ref, sem)
            copy.start()
            copy.wait()


def place(meta, others, out):
    flat = sum(others, [])
    sizes = [[part.shape[0] for part in one] for one in others]
    return pl.pallas_call(
        functools.partial(place_kernel, sizes),
        out_shape=jax.ShapeDtypeStruct(out.shape, out.dtype),
        in_specs=[SMEM] + [ANY] * len(flat) + [HBM],
        out_specs=HBM,
        scratch_shapes=[pltpu.VMEM(out.shape, out.dtype), pltpu.SemaphoreType.DMA],
        input_output_aliases={len(flat) + 1: 0},
        compiler_params=pltpu.CompilerParams(vmem_limit_bytes=6 * MIB),
        cost_estimate=pl.CostEstimate(flops=0, bytes_accessed=4 * MIB, transcendentals=0),
        name="place",
    )(meta, *flat, out)


def late_kernel(span, n_cross, final, far_ref, meta_ref, tiles_ref, acc_ref, resid_ref, w1_ref, w2_ref, *refs):
    crosses = refs[:n_cross]
    out_ref, cacc, tb, t_sem, *more_refs = refs[n_cross + (1 if final and span else 0) :]
    obuf = more_refs[0] if final else out_ref
    blk_rows, tile_len, feat = cacc.shape
    n_tiles = tiles_ref.shape[2]
    total = jnp.minimum(far_ref[span, 2, 0], tb.shape[0])

    def tile_copy(k):
        e = far_ref[span, 0, k]
        return pltpu.make_async_copy(tiles_ref.at[span, e // n_tiles, e % n_tiles], tb.at[k], t_sem.at[k])

    def start_tile(k, carry):
        tile_copy(k).start()
        return carry

    lax.fori_loop(0, total, start_tile, 0)
    cacc[...] = jnp.zeros_like(cacc)

    def one_entry(k, carry):
        row = far_ref[span, 0, k] // n_tiles
        block = far_ref[span, 1, k]
        tile_copy(k).wait()
        for c, src in enumerate(crosses):

            @pl.when((len(crosses) == 1) | (block // blk_rows == c))
            def _():
                cacc[row] += jnp.dot(tb[k], src[block - c * blk_rows], preferred_element_type=jnp.float32)

        return carry

    lax.fori_loop(0, total, one_entry, 0)
    step = 2

    def one_part(i, carry):
        rows = pl.ds(i * step, step)
        first = (resid_ref.shape[0] // blk_rows - 1) * span * blk_rows
        from_rows = pl.ds(first + i * step, step)
        agg = (acc_ref[rows] + cacc[rows]).reshape(step * tile_len, feat).astype(jnp.bfloat16)
        hidden = jnp.dot(agg, w1_ref[...], preferred_element_type=jnp.float32)
        hidden = jnp.maximum(hidden, 0.0).astype(jnp.bfloat16)
        more = jnp.dot(hidden, w2_ref[...], preferred_element_type=jnp.float32)
        more = more.reshape(step, tile_len, feat)
        obuf[rows] = (resid_ref[from_rows].astype(jnp.float32) + more).astype(jnp.bfloat16)
        if final:
            dst = out_ref.at[pl.ds(span * blk_rows + i * step, step)]
            pltpu.make_async_copy(obuf.at[rows], dst, more_refs[1]).start()
        return carry

    parts = jnp.where(meta_ref[3] != 0, blk_rows // step, 0)
    lax.fori_loop(0, parts, one_part, 0)
    if final:

        @pl.when(meta_ref[3] != 0)
        def _():
            pltpu.make_async_copy(obuf, out_ref.at[pl.ds(span * blk_rows, blk_rows)], more_refs[1]).wait()


def early(span, near, tiles, srcs):
    _, blk_rows, n_tiles, tile_len, _ = tiles.shape
    feat = srcs[0].shape[-1]
    n_src = len(srcs)
    return pl.pallas_call(
        functools.partial(early_kernel, span, n_src),
        out_shape=jax.ShapeDtypeStruct((blk_rows, tile_len, feat), jnp.float32),
        in_specs=[SMEM, ANY] + [ANY] * n_src,
        out_specs=VMEM,
        scratch_shapes=[
            pltpu.VMEM((2 * (span + 1) * blk_rows, tile_len, feat), jnp.bfloat16),
            pltpu.VMEM((blk_rows, n_tiles, tile_len, tile_len), jnp.bfloat16),
            pltpu.SemaphoreType.DMA((n_src,)),
            pltpu.SemaphoreType.DMA,
        ],
        compiler_params=pltpu.CompilerParams(vmem_limit_bytes=14 * MIB),
        cost_estimate=pl.CostEstimate(
            flops=2 * blk_rows * n_tiles * tile_len * tile_len * feat,
            bytes_accessed=8 * MIB,
            transcendentals=0,
        ),
    )(near, tiles, *srcs)


FAR = 8


def late(span, far, meta, tiles, acc, resid, crosses, weights, final=False, prior=None):
    spans, blk_rows, _, tile_len, _ = tiles.shape
    feat = acc.shape[-1]
    tail = [] if prior is None else [prior]
    args = [far, meta, tiles, acc, resid, *weights, *crosses, *tail]
    out_rows = spans * blk_rows if final else blk_rows
    return pl.pallas_call(
        functools.partial(late_kernel, span, len(crosses), final),
        out_shape=jax.ShapeDtypeStruct((out_rows, tile_len, feat), jnp.bfloat16),
        in_specs=[SMEM, SMEM, ANY] + [VMEM] * (4 + len(crosses)) + [HBM] * len(tail),
        out_specs=HBM if final else VMEM,
        scratch_shapes=[
            pltpu.VMEM((blk_rows, tile_len, feat), jnp.float32),
            pltpu.VMEM((FAR, tile_len, tile_len), jnp.bfloat16),
            pltpu.SemaphoreType.DMA((FAR,)),
        ]
        + ([pltpu.VMEM((blk_rows, tile_len, feat), jnp.bfloat16), pltpu.SemaphoreType.DMA] if final else []),
        compiler_params=pltpu.CompilerParams(vmem_limit_bytes=14 * MIB),
        input_output_aliases={len(args) - 1: 0} if tail else {},
        cost_estimate=pl.CostEstimate(
            flops=4 * blk_rows * tile_len * feat * feat,
            bytes_accessed=8 * MIB,
            transcendentals=0,
        ),
    )(*args)


def after(value, *deps):
    return lax.optimization_barrier((value, *deps))[0]


def on_device(features, tiles, w_first, w_second, tile_block):
    spans, row_count, feat = features.shape
    _, blk_rows, _, tile_len, _ = tiles.shape
    parts = lax.axis_size("dom")
    section = lax.axis_index("section")
    me = lax.axis_index("dom")
    hub = lax.axis_size("section") - 1
    row_parts = parts // 4
    z = me // row_parts
    swap_pairs = [(p, p ^ 1) for p in range(parts)]
    cross_pairs = [(p, (p + 1) % parts if p % 2 else (p - 1) % parts) for p in range(parts)]

    def swap(value):
        return lax.ppermute(value, "dom", swap_pairs)

    def cross(value):
        return lax.ppermute(value, "dom", cross_pairs)

    def hop(value, pairs):
        return lax.ppermute(value, "section", pairs)

    def along_z(value, by):
        return lax.ppermute(value, "dom", [(p, (p + by * row_parts) % parts) for p in range(parts)])

    def sums(span, h, chip):
        return early(span, near, tiles, h[: span + 1] + chip[: span + 1])

    w_first, w_second = w_first[0], w_second[0]

    def meta(mode, active):
        return jnp.stack([z, mode + me % 2, section, active.astype(jnp.int32)]).astype(jnp.int32)

    is_hub = section == hub
    metas = [
        meta(jnp.where(section == 0, 0, jnp.where(is_hub, 4, 2)), section != 2),
        meta(jnp.where(section == 1, 0, 2), (section == 1) | is_hub),
        meta(jnp.zeros_like(me), is_hub),
        meta(jnp.zeros_like(me), is_hub),
    ]

    def layer(num, acc, h, over, weights):
        out, chip_out, over_out = [], [], []
        for s in range(spans):
            out.append(late(s, far, metas[num], tiles, acc[s], h[s], over[: s + 1], weights))
            chip_out.append(swap(out[s]))
            over_out.append(cross(out[s]))
        return out, chip_out, over_out, [sums(s, out, chip_out) for s in range(spans)]

    shard, rest = mine(metas[3], w_first, w_second, [[(0, 0, CUT // 4)], [(0, 2, CUT // 4), (CUT, None, feat - CUT)]])
    shard = hop(shard, [(0, hub)])
    zero_b = hop(rest, [(0, hub)])
    mine_a, mine_b = mine(metas[3], w_first, w_second, [[(0, None, feat // 2)], [(feat // 2, None, feat // 2)]])
    start = features.reshape(spans * blk_rows, tile_len, feat)
    chip0 = swap(start)
    over0 = [cross(start[s * blk_rows : (s + 1) * blk_rows]) for s in range(spans)]
    next_a = hop(mine_a, [(0, 1), (1, 2), (2, hub)])
    zero_a = join(shard, along_z(shard, 1), along_z(shard, -1))
    next_b = hop(mine_b, [(0, 1)])
    ids = lax.dynamic_slice_in_dim(tile_block, me * blk_rows, blk_rows, 1)
    near, far = entry_tables(ids, me, parts, parts * blk_rows)
    near, far, *metas = lax.optimization_barrier((near, far, *metas))

    acc = [sums(s, [start], [chip0]) for s in range(spans)]
    one_a = hop(after(next_a, *acc), [(2, hub)])
    one_b = hop(after(mine_b, *acc), [(1, hub)])
    two_b = hop(after(mine_b, *acc), [(2, hub)])
    kept = [mine_a, mine_b, swap(mine_a), swap(mine_b)]
    swap_next = [swap(next_a), swap(next_b)]
    swap_zero = [swap(zero_a), swap(zero_b)]
    got = [*kept, next_a, next_b, *swap_next, zero_a, zero_b, *swap_zero]
    h1, _, over1, acc = layer(0, acc, [start] * spans, over0, pick(metas[0], got))
    one_a, one_b = after(one_a, h1[1]), after(one_b, h1[1])
    got = [*kept, one_a, one_b, swap(one_a), swap(one_b)]
    weights = pick(metas[1], got)

    h2, _, over2, acc = layer(1, acc, h1, over1, weights)
    two_b = after(two_b, h2[1])
    got = [next_a, two_b, swap_next[0], swap(two_b)]
    weights = pick(metas[2], got)

    h3, _, over3, acc = layer(2, acc, h2, over2, weights)
    back = [hop(h3[s], [(hub, 2)]) for s in range(spans)]

    out = None
    for s in range(spans):
        out = late(s, far, metas[3], tiles, acc[s], h3[s], over3[: s + 1], [w_first, w_second], True, out)
    out = place(metas[3], [h1, h2, back], out)
    return out.reshape(1, spans, row_count, feat)


def solution(mesh):
    placed = (
        P(None, "dom", None),
        P(None, "dom", None, None, None),
        P("section", None, None),
        P("section", None, None),
        P(),
    )
    return jax.shard_map(
        on_device,
        mesh=mesh,
        in_specs=placed,
        out_specs=P("section", None, "dom", None),
        check_vma=False,
    )
```

```python
import functools

import jax
import jax.numpy as jnp
from jax import lax
from jax.experimental import pallas as pl
from jax.experimental.pallas import tpu as pltpu
from jax.sharding import PartitionSpec as P


ANY = pl.BlockSpec(memory_space=pl.ANY)
SMEM = pl.BlockSpec(memory_space=pltpu.SMEM)
VMEM = pl.BlockSpec(memory_space=pltpu.VMEM)
HBM = pl.BlockSpec(memory_space=pltpu.HBM)
MIB = 2**20


def entry_tables(ids, me, parts, nbc):
    spans, blk_rows, n_tiles = ids.shape
    count = blk_rows * n_tiles
    ids = ids.reshape(spans, count)
    within = ids % nbc
    rel = (within // blk_rows - me + parts) % parts
    local = ids // nbc * blk_rows + within % blk_rows
    on_chip = jnp.where(me % 2 == 0, 1, parts - 1)
    across = (rel != 0) & (rel != on_chip)
    held = (1 + jnp.arange(spans, dtype=jnp.int32)[:, None]) * blk_rows
    slot = jnp.where(across, 0, jnp.where(rel == on_chip, held + local, local))
    near = jnp.stack([slot, jnp.where(across, 0, 1)], axis=1).astype(jnp.int32)
    order = jnp.arange(count, dtype=jnp.int32)
    before = (order[None, :] < order[:, None])[None]
    rank = jnp.sum(jnp.where(before & across[:, None, :], 1, 0), axis=2)
    chosen = across[:, None, :] & (rank[:, None, :] == order[None, :, None])
    place = jnp.sum(jnp.where(chosen, order[None, None, :], 0), axis=2)
    block = jnp.sum(jnp.where(chosen, local[:, None, :], 0), axis=2)
    total = jnp.sum(jnp.where(across, 1, 0), axis=1, keepdims=True) + jnp.zeros_like(place)
    far = jnp.stack([place, block, total], axis=1).astype(jnp.int32)
    return near, far


def early_kernel(span, n_src, near_ref, tiles_ref, *refs):
    srcs = refs[:n_src]
    acc_ref, buf, tbuf, src_sem, tile_sem = refs[n_src:]
    blk_rows, n_tiles, _, _ = tbuf.shape
    copies = [pltpu.make_async_copy(tiles_ref.at[span], tbuf, tile_sem)]
    for i, src in enumerate(srcs):
        size = buf.shape[0] // n_src
        rows = pl.ds(i * size, size)
        copies.append(pltpu.make_async_copy(src.at[pl.ds(0, size)], buf.at[rows], src_sem.at[i]))
    for copy in copies:
        copy.start()
    for copy in copies:
        copy.wait()

    def one_row(row, carry):
        total = None
        for pair in range(n_tiles // 2):
            lhs, rhs = [], []
            for j in (2 * pair, 2 * pair + 1):
                e = row * n_tiles + j
                tile = tbuf[row, j]
                lhs.append(jnp.where(near_ref[span, 1, e] == 0, jnp.zeros_like(tile), tile))
                rhs.append(buf[near_ref[span, 0, e]])
            part = jnp.dot(
                jnp.concatenate(lhs, axis=1),
                jnp.concatenate(rhs, axis=0),
                preferred_element_type=jnp.float32,
            )
            total = part if total is None else total + part
        acc_ref[row] = total
        return carry

    lax.fori_loop(0, blk_rows, one_row, 0)


def pick_kernel(n_got, pieced, meta_ref, *refs):
    got_refs = refs[:n_got]
    w1_ref, w2_ref, sem = refs[n_got:]
    feat = w1_ref.shape[0]
    mid = feat // 2
    mode = meta_ref[1]

    def fetch(one, two):
        for part, dst, k in ((one, w1_ref, 0), (two, w2_ref, 1)):
            for src, rows in part:
                pltpu.make_async_copy(src, dst.at[rows], sem.at[k]).start()

    def halves(a, b):
        return [(a, pl.ds(0, mid)), (b, pl.ds(mid, mid))]

    def shards(a, b):
        z = meta_ref[0]
        quarter = a.shape[0] // 3
        part = []
        for src, k, away in ((a, 0, 0), (a, 1, 3), (a, 2, 1), (b, 0, 2)):
            start = pl.multiple_of((z + away) % 4 * quarter, quarter)
            part.append((src.at[pl.ds(k * quarter, quarter)], pl.ds(start, quarter)))
        size = feat - 4 * quarter
        return part + [(b.at[pl.ds(quarter, size)], pl.ds(4 * quarter, size))]

    choices = []
    for at in range(0, n_got, 4):
        form = shards if pieced and at else halves
        one, two = form(*got_refs[at : at + 2]), form(*got_refs[at + 2 : at + 4])
        choices += [(at // 2, one, two), (at // 2 + 1, two, one)]
    for value, one, two in choices:
        pl.when(mode == value)(functools.partial(fetch, one, two))
    pltpu.make_async_copy(w1_ref, w1_ref, sem.at[0]).wait()
    pltpu.make_async_copy(w2_ref, w2_ref, sem.at[1]).wait()


def pick(meta, got, pieced=False):
    feat = got[0].shape[-1]
    shape = jax.ShapeDtypeStruct((feat, feat), jnp.bfloat16)
    return list(
        pl.pallas_call(
            functools.partial(pick_kernel, len(got), pieced),
            out_shape=[shape, shape],
            in_specs=[SMEM] + [ANY] * len(got),
            out_specs=[VMEM, VMEM],
            scratch_shapes=[pltpu.SemaphoreType.DMA((2,))],
            compiler_params=pltpu.CompilerParams(vmem_limit_bytes=6 * MIB),
            cost_estimate=pl.CostEstimate(flops=0, bytes_accessed=8 * MIB, transcendentals=0),
            name="pick",
        )(meta, *got)
    )


CUT = 768


def mine_kernel(pieces, meta_ref, first_ref, second_ref, *refs):
    *outs, sem = refs

    def fetch(src):
        for k, (ranges, dst) in enumerate(zip(pieces, outs)):
            at = 0
            for start, away, size in ranges:
                if away is not None:
                    start = pl.multiple_of((meta_ref[0] + away) % 4 * size, size)
                pltpu.make_async_copy(src.at[pl.ds(start, size)], dst.at[pl.ds(at, size)], sem.at[k]).start()
                at += size

    pl.when(meta_ref[1] == 0)(functools.partial(fetch, first_ref))
    pl.when(meta_ref[1] != 0)(functools.partial(fetch, second_ref))
    for k, dst in enumerate(outs):
        pltpu.make_async_copy(dst, dst, sem.at[k]).wait()


def mine(meta, w_first, w_second, pieces):
    feat = w_first.shape[0]
    shapes = [jax.ShapeDtypeStruct((sum(r[2] for r in one), feat), jnp.bfloat16) for one in pieces]
    return pl.pallas_call(
        functools.partial(mine_kernel, pieces),
        out_shape=shapes,
        in_specs=[SMEM, HBM, HBM],
        out_specs=[VMEM] * len(pieces),
        scratch_shapes=[pltpu.SemaphoreType.DMA((len(pieces),))],
        compiler_params=pltpu.CompilerParams(vmem_limit_bytes=52 * MIB),
        cost_estimate=pl.CostEstimate(flops=0, bytes_accessed=4 * MIB, transcendentals=0),
        name="mine",
    )(meta, w_first, w_second)


def choose_kernel(meta_ref, one_ref, two_ref, out_ref, sem):
    for use, src in ((meta_ref[2] != 1, one_ref), (meta_ref[2] == 1, two_ref)):
        pl.when(use)(pltpu.make_async_copy(src, out_ref, sem).start)
    pltpu.make_async_copy(out_ref, out_ref, sem).wait()


def choose(meta, one, two):
    return pl.pallas_call(
        choose_kernel,
        out_shape=jax.ShapeDtypeStruct(one.shape, one.dtype),
        in_specs=[SMEM, ANY, ANY],
        out_specs=VMEM,
        scratch_shapes=[pltpu.SemaphoreType.DMA],
        compiler_params=pltpu.CompilerParams(vmem_limit_bytes=4 * MIB),
        cost_estimate=pl.CostEstimate(flops=0, bytes_accessed=MIB, transcendentals=0),
        name="choose",
    )(meta, one, two)


def join_kernel(*refs):
    *parts, out_ref, sem = refs
    size = parts[0].shape[0]
    for k, part in enumerate(parts):
        pltpu.make_async_copy(part, out_ref.at[pl.ds(k * size, size)], sem).start()
    pltpu.make_async_copy(out_ref, out_ref, sem).wait()


def join(*parts):
    size, feat = parts[0].shape
    return pl.pallas_call(
        join_kernel,
        out_shape=jax.ShapeDtypeStruct((len(parts) * size, feat), jnp.bfloat16),
        in_specs=[ANY] * len(parts),
        out_specs=VMEM,
        scratch_shapes=[pltpu.SemaphoreType.DMA],
        compiler_params=pltpu.CompilerParams(vmem_limit_bytes=4 * MIB),
        cost_estimate=pl.CostEstimate(flops=0, bytes_accessed=2 * MIB, transcendentals=0),
        name="join",
    )(*parts)


def place_kernel(sizes, meta_ref, *refs):
    count = sum(len(one) for one in sizes)
    others = refs[:count]
    out_ref, buf, sem = refs[count + 1 :]
    at = 0
    for k, one in enumerate(sizes):
        mine_refs = others[at : at + len(one)]
        at += len(one)

        @pl.when(meta_ref[2] == k)
        def _():
            start = 0
            for src, size in zip(mine_refs, one):
                pltpu.make_async_copy(src, buf.at[pl.ds(start, size)], sem).start()
                start += size
            pltpu.make_async_copy(buf, buf, sem).wait()
            copy = pltpu.make_async_copy(buf, out_ref, sem)
            copy.start()
            copy.wait()


def place(meta, others, out):
    flat = sum(others, [])
    sizes = [[part.shape[0] for part in one] for one in others]
    return pl.pallas_call(
        functools.partial(place_kernel, sizes),
        out_shape=jax.ShapeDtypeStruct(out.shape, out.dtype),
        in_specs=[SMEM] + [ANY] * len(flat) + [HBM],
        out_specs=HBM,
        scratch_shapes=[pltpu.VMEM(out.shape, out.dtype), pltpu.SemaphoreType.DMA],
        input_output_aliases={len(flat) + 1: 0},
        compiler_params=pltpu.CompilerParams(vmem_limit_bytes=6 * MIB),
        cost_estimate=pl.CostEstimate(flops=0, bytes_accessed=4 * MIB, transcendentals=0),
        name="place",
    )(meta, *flat, out)


def late_kernel(span, n_cross, final, far_ref, meta_ref, tiles_ref, acc_ref, resid_ref, w1_ref, w2_ref, *refs):
    crosses = refs[:n_cross]
    out_ref, cacc, tb, t_sem, *more_refs = refs[n_cross + (1 if final and span else 0) :]
    obuf = more_refs[0] if final else out_ref
    blk_rows, tile_len, feat = cacc.shape
    n_tiles = tiles_ref.shape[2]
    total = jnp.minimum(far_ref[span, 2, 0], tb.shape[0])

    def tile_copy(k):
        e = far_ref[span, 0, k]
        return pltpu.make_async_copy(tiles_ref.at[span, e // n_tiles, e % n_tiles], tb.at[k], t_sem.at[k])

    def start_tile(k, carry):
        tile_copy(k).start()
        return carry

    lax.fori_loop(0, total, start_tile, 0)
    cacc[...] = jnp.zeros_like(cacc)

    def one_entry(k, carry):
        row = far_ref[span, 0, k] // n_tiles
        block = far_ref[span, 1, k]
        tile_copy(k).wait()
        for c, src in enumerate(crosses):

            @pl.when((len(crosses) == 1) | (block // blk_rows == c))
            def _():
                cacc[row] += jnp.dot(tb[k], src[block - c * blk_rows], preferred_element_type=jnp.float32)

        return carry

    lax.fori_loop(0, total, one_entry, 0)
    step = 2

    def one_part(i, carry):
        rows = pl.ds(i * step, step)
        first = (resid_ref.shape[0] // blk_rows - 1) * span * blk_rows
        from_rows = pl.ds(first + i * step, step)
        agg = (acc_ref[rows] + cacc[rows]).reshape(step * tile_len, feat).astype(jnp.bfloat16)
        hidden = jnp.dot(agg, w1_ref[...], preferred_element_type=jnp.float32)
        hidden = jnp.maximum(hidden, 0.0).astype(jnp.bfloat16)
        more = jnp.dot(hidden, w2_ref[...], preferred_element_type=jnp.float32)
        more = more.reshape(step, tile_len, feat)
        obuf[rows] = (resid_ref[from_rows].astype(jnp.float32) + more).astype(jnp.bfloat16)
        if final:
            dst = out_ref.at[pl.ds(span * blk_rows + i * step, step)]
            pltpu.make_async_copy(obuf.at[rows], dst, more_refs[1]).start()
        return carry

    parts = jnp.where(meta_ref[3] != 0, blk_rows // step, 0)
    lax.fori_loop(0, parts, one_part, 0)
    if final:

        @pl.when(meta_ref[3] != 0)
        def _():
            pltpu.make_async_copy(obuf, out_ref.at[pl.ds(span * blk_rows, blk_rows)], more_refs[1]).wait()


def early(span, near, tiles, srcs):
    _, blk_rows, n_tiles, tile_len, _ = tiles.shape
    feat = srcs[0].shape[-1]
    n_src = len(srcs)
    return pl.pallas_call(
        functools.partial(early_kernel, span, n_src),
        out_shape=jax.ShapeDtypeStruct((blk_rows, tile_len, feat), jnp.float32),
        in_specs=[SMEM, ANY] + [ANY] * n_src,
        out_specs=VMEM,
        scratch_shapes=[
            pltpu.VMEM((2 * (span + 1) * blk_rows, tile_len, feat), jnp.bfloat16),
            pltpu.VMEM((blk_rows, n_tiles, tile_len, tile_len), jnp.bfloat16),
            pltpu.SemaphoreType.DMA((n_src,)),
            pltpu.SemaphoreType.DMA,
        ],
        compiler_params=pltpu.CompilerParams(vmem_limit_bytes=14 * MIB),
        cost_estimate=pl.CostEstimate(
            flops=2 * blk_rows * n_tiles * tile_len * tile_len * feat,
            bytes_accessed=8 * MIB,
            transcendentals=0,
        ),
    )(near, tiles, *srcs)


FAR = 8


def late(span, far, meta, tiles, acc, resid, crosses, weights, final=False, prior=None):
    spans, blk_rows, _, tile_len, _ = tiles.shape
    feat = acc.shape[-1]
    tail = [] if prior is None else [prior]
    args = [far, meta, tiles, acc, resid, *weights, *crosses, *tail]
    out_rows = spans * blk_rows if final else blk_rows
    return pl.pallas_call(
        functools.partial(late_kernel, span, len(crosses), final),
        out_shape=jax.ShapeDtypeStruct((out_rows, tile_len, feat), jnp.bfloat16),
        in_specs=[SMEM, SMEM, ANY] + [VMEM] * (4 + len(crosses)) + [HBM] * len(tail),
        out_specs=HBM if final else VMEM,
        scratch_shapes=[
            pltpu.VMEM((blk_rows, tile_len, feat), jnp.float32),
            pltpu.VMEM((FAR, tile_len, tile_len), jnp.bfloat16),
            pltpu.SemaphoreType.DMA((FAR,)),
        ]
        + ([pltpu.VMEM((blk_rows, tile_len, feat), jnp.bfloat16), pltpu.SemaphoreType.DMA] if final else []),
        compiler_params=pltpu.CompilerParams(vmem_limit_bytes=14 * MIB),
        input_output_aliases={len(args) - 1: 0} if tail else {},
        cost_estimate=pl.CostEstimate(
            flops=4 * blk_rows * tile_len * feat * feat,
            bytes_accessed=8 * MIB,
            transcendentals=0,
        ),
    )(*args)


def after(value, *deps):
    return lax.optimization_barrier((value, *deps))[0]


def on_device(features, tiles, w_first, w_second, tile_block):
    spans, row_count, feat = features.shape
    _, blk_rows, _, tile_len, _ = tiles.shape
    parts = lax.axis_size("dom")
    section = lax.axis_index("section")
    me = lax.axis_index("dom")
    hub = lax.axis_size("section") - 1
    row_parts = parts // 4
    z = me // row_parts
    swap_pairs = [(p, p ^ 1) for p in range(parts)]
    cross_pairs = [(p, (p + 1) % parts if p % 2 else (p - 1) % parts) for p in range(parts)]

    def swap(value):
        return lax.ppermute(value, "dom", swap_pairs)

    def cross(value):
        return lax.ppermute(value, "dom", cross_pairs)

    def hop(value, pairs):
        return lax.ppermute(value, "section", pairs)

    def along_z(value, by):
        return lax.ppermute(value, "dom", [(p, (p + by * row_parts) % parts) for p in range(parts)])

    def sums(span, h, chip):
        return early(span, near, tiles, h[: span + 1] + chip[: span + 1])

    w_first, w_second = w_first[0], w_second[0]

    def meta(mode, active):
        return jnp.stack([z, mode + me % 2, section, active.astype(jnp.int32)]).astype(jnp.int32)

    is_hub = section == hub
    metas = [
        meta(jnp.where(section == 0, 0, 2), section != 2),
        meta(jnp.where(section == 1, 0, 2), (section == 1) | is_hub),
        meta(jnp.zeros_like(me), is_hub),
        meta(jnp.zeros_like(me), is_hub),
    ]

    def layer(num, acc, h, over, weights):
        out, chip_out, over_out = [], [], []
        for s in range(spans):
            out.append(late(s, far, metas[num], tiles, acc[s], h[s], over[: s + 1], weights))
            chip_out.append(swap(out[s]))
            over_out.append(cross(out[s]))
        return out, chip_out, over_out, [sums(s, out, chip_out) for s in range(spans)]

    shard, rest = mine(metas[3], w_first, w_second, [[(0, 0, CUT // 4)], [(0, 2, CUT // 4), (CUT, None, feat - CUT)]])
    shard = choose(metas[3], hop(shard, [(0, hub)]), hop(shard, [(0, 1)]))
    zero_b = [hop(rest, [(0, hub)]), hop(rest, [(0, 1)])]
    mine_a, mine_b = mine(metas[3], w_first, w_second, [[(0, None, feat // 2)], [(feat // 2, None, feat // 2)]])
    start = features.reshape(spans * blk_rows, tile_len, feat)
    chip0 = swap(start)
    over0 = [cross(start[s * blk_rows : (s + 1) * blk_rows]) for s in range(spans)]
    next_a = hop(mine_a, [(1, 2), (2, hub)])
    zero_a = join(shard, along_z(shard, 1), along_z(shard, -1))
    ids = lax.dynamic_slice_in_dim(tile_block, me * blk_rows, blk_rows, 1)
    near, far = entry_tables(ids, me, parts, parts * blk_rows)
    near, far, *metas = lax.optimization_barrier((near, far, *metas))

    acc = [sums(s, [start], [chip0]) for s in range(spans)]
    one_a = hop(after(next_a, *acc), [(2, hub)])
    one_b = hop(after(mine_b, *acc), [(1, hub)])
    two_b = hop(after(mine_b, *acc), [(2, hub)])
    kept = [mine_a, mine_b, swap(mine_a), swap(mine_b)]
    zero_b = choose(metas[3], *after(tuple(zero_b), *acc))
    swap_zero = [swap(zero_a), swap(zero_b)]
    got = [*kept, zero_a, zero_b, *swap_zero]
    h1, _, over1, acc = layer(0, acc, [start] * spans, over0, pick(metas[0], got, True))
    one_a, one_b = after(one_a, h1[1]), after(one_b, h1[1])
    got = [*kept, one_a, one_b, swap(one_a), swap(one_b)]
    weights = pick(metas[1], got)

    h2, _, over2, acc = layer(1, acc, h1, over1, weights)
    two_b = after(two_b, h2[1])
    got = [next_a, two_b, swap(after(next_a, h2[1])), swap(two_b)]
    weights = pick(metas[2], got)

    h3, _, over3, acc = layer(2, acc, h2, over2, weights)
    back = [hop(h3[s], [(hub, 2)]) for s in range(spans)]

    out = None
    for s in range(spans):
        out = late(s, far, metas[3], tiles, acc[s], h3[s], over3[: s + 1], [w_first, w_second], True, out)
    out = place(metas[3], [h1, h2, back], out)
    return out.reshape(1, spans, row_count, feat)


def solution(mesh):
    placed = (
        P(None, "dom", None),
        P(None, "dom", None, None, None),
        P("section", None, None),
        P("section", None, None),
        P(),
    )
    return jax.shard_map(
        on_device,
        mesh=mesh,
        in_specs=placed,
        out_specs=P("section", None, "dom", None),
        check_vma=False,
    )
```
